512 devices in a mesh: seq: 128 (over x, z, y_hi, core), head: 4 (over y_lo).
Axes of the slice: x: 4, y: 8 (y_hi: 2, y_lo: 4; y = y_hi * 4 + y_lo), z: 8, core: 2. Of those that a mesh axis runs over, the one named last changes fastest.
Arguments:
- queries: bfloat16 [16384, 512], P('seq'), may hold values from -52 to 52
- source: bfloat16 [16384, 512], P('seq'), may hold values from -6 to 6
- order: int32 [16384], P('seq'), may hold values from 0 to 127, as said below
- avail: int32 [16384], P('seq'), may hold values from 0 to 1, as said below
- pos_table: bfloat16 [16384, 2, 512], P('seq', None, 'head'), may hold values from -6 to 6
- w_query: bfloat16 [512, 512], P(None, 'head'), may hold values from -0.25 to 0.25
- w_keyval: bfloat16 [512, 2, 512], P(None, None, 'head'), may hold values from -0.25 to 0.25
- w_out: bfloat16 [512, 512], P('head'), may hold values from -0.25 to 0.25
Outputs:
- joined: bfloat16 [16384, 512], P('seq', 'head')
The draws below stay inside these ranges and needn't reach their ends.
Inputs may be any that keep to these rules, and one draw needn't show every extreme that they name: `order`: each aligned block of 128 entries is a permutation of 0 to 127. `avail`: every aligned block of 8 entries holds at least one 1.
All inputs are finite; a program needn't handle non-finite values.
Results may differ from the reference program's by a relative error of at most 0.0085.
Values may be sent and summed in bfloat16 or wider, within the bound.
No kernel may reach another device: no remote copies, remote signals or barrier semaphores. Data moves between devices by JAX's collectives and lax.ppermute only.
A program may use at most 128 MiB of HBM per device.

```python
import jax
import jax.numpy as jnp
from jax import lax

D = 512
HEADS = 8
HD = 64
SRC_DEV = 128
QTOKENS = 16384
SOURCE = 16384
N_SEQ = 128


def draw_queries(key, part):
    shape = (QTOKENS, D)
    return jnp.clip(jax.random.normal(key, shape, jnp.float32), -4.0, 4.0).astype(jnp.bfloat16)


def draw_order(key, part):
    blocks = SOURCE // SRC_DEV
    keys = jax.random.split(jax.random.fold_in(key, 23), blocks)
    perms = jax.vmap(lambda single: jax.random.permutation(single, SRC_DEV))(keys)
    return perms.reshape(SOURCE).astype(jnp.int32)


def draw_avail(key, part):
    rows = SOURCE // 8
    coins = jax.random.randint(jax.random.fold_in(key, 31), (rows, 8), 0, 4)
    forced = jax.random.randint(jax.random.fold_in(key, 37), (rows, 1), 0, 8)
    slots = jnp.arange(8, dtype=jnp.int32)[None, :]
    flags = jnp.where((coins > 0) | (slots == forced), 1, 0)
    return flags.reshape(SOURCE).astype(jnp.int32)


def steps_of(rng, extent, pieces, smallest, top_value):
    def one(dim, shards_of):
        draws = jax.random.uniform(jax.random.fold_in(jax.random.fold_in(rng, 6), dim), (shards_of,), jnp.float32, smallest / len(pieces), top_value / len(pieces))
        return jnp.repeat(jnp.exp(draws), extent[dim] // shards_of).reshape((-1,) + (1,) * (len(extent) - dim - 1))

    level = one(*pieces[0])
    for cut in pieces[1:]:
        level = level * one(*cut)
    return level


def bell_draw(stream_key, extent, scale, most, shards=(), kind=jnp.bfloat16):
    drawn = jax.random.normal(stream_key, extent, jnp.float32) * scale
    if len(shards) > 0:
        drawn = steps_of(stream_key, extent, shards, -0.22, 0.18) * drawn
    return jnp.clip(drawn, min=-most, max=most).astype(kind)


def setup_inputs(seed: int = 0) -> dict:
    streams_of = jax.random.split(jax.random.key(seed), 9)
    return {
        "queries": draw_queries(jax.random.fold_in(streams_of[8], 71), 0),
        "source": bell_draw(streams_of[1], (SOURCE, D), 1.0, 6.0, ((0, 128),)),
        "order": draw_order(jax.random.fold_in(streams_of[8], 71), 0),
        "avail": draw_avail(jax.random.fold_in(streams_of[8], 71), 0),
        "pos_table": bell_draw(streams_of[4], (SOURCE, 2, D), 1.0, 6.0, ((0, 128), (2, 4))),
        "w_query": bell_draw(streams_of[5], (D, D), D ** -0.5, 0.25, ((1, 4),)),
        "w_keyval": bell_draw(streams_of[6], (D, 2, D), D ** -0.5, 0.25, ((2, 4),)),
        "w_out": bell_draw(streams_of[7], (D, D), D ** -0.5, 0.25, ((0, 4),)),
    }


def relay(values):
    blocks = SOURCE // SRC_DEV
    group = SRC_DEV // N_SEQ
    tail = values.shape[1:]
    shaped = values.reshape((blocks, N_SEQ, group) + tail)
    return jnp.swapaxes(shaped, 0, 1).reshape((SOURCE,) + tail)


def reference(queries, source, order, avail, pos_table, w_query, w_keyval, w_out):
    blocks = SOURCE // SRC_DEV
    starts = (jnp.arange(blocks, dtype=jnp.int32) * SRC_DEV)[:, None]
    picks = (starts + order.reshape(blocks, SRC_DEV).astype(jnp.int32)).reshape(-1).astype(jnp.int32)
    seq_rows = relay(source[picks])
    seq_flags = relay(avail[picks])
    proj = jnp.einsum("rd,djc->rjc", seq_rows.astype(jnp.float32), w_keyval.astype(jnp.float32))
    keyval = (proj + pos_table.astype(jnp.float32)).astype(jnp.bfloat16)
    keys = keyval[:, 0].reshape(SOURCE, HEADS, HD).astype(jnp.float32)
    values = keyval[:, 1].reshape(SOURCE, HEADS, HD).astype(jnp.float32)
    query = jnp.dot(queries, w_query, preferred_element_type=jnp.float32).astype(jnp.bfloat16)
    live = (seq_flags > 0)[None, None, :]
    scale = 2.0 / (HD ** 0.5)
    width = 256 if QTOKENS % 256 == 0 else QTOKENS
    qblocks = query.reshape(QTOKENS // width, width, HEADS, HD)

    def attend(qblock):
        score = jnp.einsum("qhe,khe->hqk", qblock.astype(jnp.float32), keys) * scale
        score = jnp.where(live, score, jnp.float32(-1e30))
        top = jnp.max(score, axis=-1, keepdims=True)
        weight = jnp.where(live, jnp.exp(score - top), jnp.float32(0.0))
        total = jnp.sum(weight, axis=-1)
        rounded = lax.optimization_barrier(weight.astype(jnp.bfloat16))
        summed = jnp.einsum("hqk,khe->hqe", rounded.astype(jnp.float32), values)
        result = summed / total[..., None]
        return jnp.transpose(result, (1, 0, 2)).reshape(width, D).astype(jnp.bfloat16)

    attn = lax.map(attend, qblocks).reshape(QTOKENS, D)
    mixed = queries.astype(jnp.float32) + jnp.dot(attn, w_out, preferred_element_type=jnp.float32)
    return mixed.astype(jnp.bfloat16)
```

```python
import functools

import jax
import jax.numpy as jnp
from jax import lax
from jax.experimental import pallas as pl
from jax.experimental.pallas import tpu as pltpu
from jax.sharding import Mesh
from jax.sharding import PartitionSpec as P

HD = 64
SPLIT = (("x", 4), ("zh", 4), ("zl", 2), ("yh", 2), ("c", 2))
SEQ = tuple(n for n, _ in SPLIT)
I = ("zh", "yh")
J = ("x", "zl")
NI = 8
NJ = 8
BIG = 1048576.0
CUT = 65536.0
NEG = -1e30
F32 = jnp.float32
BF16 = jnp.bfloat16


def seq_of(i, j, c):
    size = dict(SPLIT)
    part = {"c": c}
    for names, index in ((I, i), (J, j)):
        for name in reversed(names):
            part[name] = index % size[name]
            index = index // size[name]
    place = 0
    for name, n in SPLIT:
        place = place * n + part[name]
    return place


def iota(shape, dim):
    return lax.broadcasted_iota(jnp.int32, shape, dim)


def onehot(mask):
    return jnp.where(mask, F32(1.0), F32(0.0)).astype(BF16)


def mm(a, b, ca=1, cb=0):
    return lax.dot_general(a, b, (((ca,), (cb,)), ((), ())), preferred_element_type=F32)


def split_kernel(pos_ref, out_ref):
    row, col = iota((128, 128), 0), iota((128, 128), 1)
    relay = onehot(col == seq_of(row // 16, row % 8, (row // 8) % 2))
    for part in range(2):
        out_ref[:, part * 8 : part * 8 + 8, :] = (
            mm(relay, pos_ref[:, part, :]).astype(BF16).reshape(2 * NI, NJ, 128)
        )


def pack_kernel(source_ref, order_ref, avail_ref, queries_ref, wq_ref, out_ref):
    row, col = iota((128, 128), 0), iota((128, 128), 1)
    pick = onehot(jnp.broadcast_to(order_ref[...], (128, 128)) == row)
    relay = onehot(row == seq_of((col // 2) % NI, col // 16, col % 2))
    pick = mm(pick, relay).astype(BF16)
    avail = jnp.broadcast_to(avail_ref[...], (128, 128))
    diag = onehot((row == col) & (avail > 0))
    flags = mm(diag, jnp.ones((128, 512), BF16)).astype(BF16)
    live = mm(pick, flags, 0, 0) > 0.5
    rows = jnp.where(live, mm(pick, source_ref[...], 0, 0), F32(BIG)).astype(BF16)
    q = mm(queries_ref[...], wq_ref[...]).astype(BF16)
    q = (q.astype(F32) * (2.0 / HD**0.5)).astype(BF16)
    for j in range(NJ):
        for part in range(4):
            out_ref[j, part * 16 : part * 16 + 16, :] = rows[
                j * 16 : j * 16 + 16, part * 128 : part * 128 + 128
            ]
        out_ref[j, 64:192, :] = q


def project_kernel(got_ref, pos_ref, wk_ref, wv_ref, out_ref):
    parts = [got_ref[:, part * 16 : part * 16 + 16, :].reshape(128, 128) for part in range(4)]
    live = parts[0].astype(F32) < CUT
    rows = jnp.concatenate(parts, axis=1)
    row, col = iota((128, 128), 0), iota((128, 128), 1)
    relay = onehot(col == (row % 16) * 8 + row // 16)
    for part, w_ref, mark in ((0, wk_ref, BIG), (1, wv_ref, 0.0)):
        pos = pos_ref[:, part * 8 : part * 8 + 8, :].reshape(128, 128)
        out = mm(rows, w_ref[...]) + mm(relay, pos)
        out = jnp.where(live, out, F32(mark)).astype(BF16)
        for i in range(NI):
            out_ref[i, part] = out


def attend_kernel(got_ref, own_ref, other_ref, out_ref, kaug_ref, vaug_ref, *, qb):
    n = NI * 128
    lane = iota((n, 128), 1)
    for side, ref in ((0, own_ref), (1, other_ref)):
        keys = ref[:, 0].reshape(n, 128).astype(F32)
        values = ref[:, 1].reshape(n, 128).astype(F32)
        bad = keys > CUT
        for h in range(2):
            mark = lane == 64 * (1 - h)
            kaug_ref[h, side * n : side * n + n] = jnp.where(
                mark, jnp.where(bad, F32(NEG), F32(0.0)), jnp.where(bad, F32(0.0), keys)
            ).astype(BF16)
            mine = (lane >= 64) if h else (lane < 64)
            vaug_ref[h, side * n : side * n + n] = jnp.where(mine, values, F32(1.0)).astype(BF16)

    lane = iota((qb, 128), 1)
    erow, ecol = iota((16, 128), 0), iota((16, 128), 1)
    pull = onehot((erow < 6) & (ecol == erow % 3 + 64 * (erow // 3)))
    per = qb // 128

    def block(t, carry):
        q = got_ref[pl.ds(t * per, per), 64:192, :].reshape(qb, 128).astype(F32)
        sums, tops = [], []
        for h in range(2):
            mine = (lane >= 64) if h else (lane < 64)
            qh = jnp.where(mine, q, jnp.where(lane == 64 * (1 - h), F32(1.0), F32(0.0)))
            score = mm(qh.astype(BF16), kaug_ref[h], 1, 1)
            top = jnp.max(score, axis=1, keepdims=True)
            weight = jnp.exp(score - top).astype(BF16)
            sums.append(mm(weight, vaug_ref[h]))
            tops.append(top)
        low = lane < 64
        summed = jnp.where(low, sums[0], sums[1])
        total = pltpu.roll(jnp.where(low, sums[1], sums[0]), 64, 1)
        mean = (summed / total).astype(BF16)
        lse = jnp.where(low, tops[0], tops[1]) + jnp.log(total)
        hi = lse.astype(BF16).astype(F32)
        mid = (lse - hi).astype(BF16).astype(F32)
        tail = lse - hi - mid
        which = lane % 64
        piece = jnp.where(which == 0, hi, jnp.where(which == 1, mid, tail)).astype(BF16)
        for u in range(per):
            out_ref[t * per + u, 0:128, :] = mean[u * 128 : u * 128 + 128]
            out_ref[t * per + u, 128:144, :] = mm(pull, piece[u * 128 : u * 128 + 128], 1, 1).astype(BF16)
        return carry

    lax.fori_loop(0, NJ // per, block, 0)


def combine_kernel(got_ref, wo_ref, out_ref):
    row, col = iota((16, 128), 0), iota((16, 128), 1)
    push = onehot(((row < 3) & (col < 64)) | ((row >= 3) & (row < 6) & (col >= 64)))
    lse = [mm(got_ref[j, 128:144, :], push, 0, 0) for j in range(NJ)]
    top = functools.reduce(jnp.maximum, lse)
    total = jnp.zeros((128, 128), F32)
    summed = jnp.zeros((128, 128), F32)
    for j in range(NJ):
        w = jnp.exp(lse[j] - top)
        total = total + w
        summed = summed + w * got_ref[j, 0:128, :].astype(F32)
    attn = (summed / total).astype(BF16)
    terms = mm(attn, wo_ref[...]).astype(BF16)
    for h in range(4):
        out_ref[h] = terms[:, h * 128 : h * 128 + 128]


def vcall(kernel, out, args, scalars=0, scratch=()):
    specs = [pl.BlockSpec(memory_space=pltpu.SMEM)] * scalars
    specs += [pl.BlockSpec(memory_space=pltpu.VMEM)] * (len(args) - scalars)
    outs = jax.tree.map(lambda _: pl.BlockSpec(memory_space=pltpu.VMEM), out)
    return pl.pallas_call(
        kernel,
        out_shape=out,
        in_specs=specs,
        out_specs=outs,
        scratch_shapes=list(scratch),
        compiler_params=pltpu.CompilerParams(vmem_limit_bytes=48 * 1024 * 1024),
    )(*args)


def bf(*shape):
    return jax.ShapeDtypeStruct(shape, BF16)


def swap(x, axes):
    return lax.all_to_all(x, axes, split_axis=0, concat_axis=0, tiled=True)


def local(queries, source, order, avail, pos_table, w_query, w_keyval, w_out):
    pos = swap(vcall(split_kernel, bf(2 * NI, 16, 128), (pos_table,)), (*I, "c"))
    packed = vcall(
        pack_kernel,
        bf(NJ, 192, 128),
        (source, order.reshape(1, 128), avail.reshape(1, 128), queries, w_query),
    )
    got = swap(packed, J)
    spread = vcall(
        project_kernel, bf(NI, 2, 128, 128), (got, pos, w_keyval[:, 0], w_keyval[:, 1])
    )
    own = swap(spread, I)
    other = lax.ppermute(own, "c", ((0, 1), (1, 0)))
    partial = vcall(
        functools.partial(attend_kernel, qb=256),
        bf(NJ, 144, 128),
        (got, own, other),
        scratch=(pltpu.VMEM((2, 2048, 128), BF16), pltpu.VMEM((2, 2048, 128), BF16)),
    )
    partial = swap(partial, J)
    terms = vcall(combine_kernel, bf(4, 128, 128), (partial, w_out))
    terms = swap(terms, "head")
    own = lax.dynamic_slice_in_dim(queries, lax.axis_index("head") * 128, 128, 1)
    return (own.astype(F32) + terms.astype(F32).sum(axis=0)).astype(BF16)


def solution(mesh):
    fine = Mesh(mesh.devices.reshape(*(n for _, n in SPLIT), 4), (*SEQ, "head"))
    in_specs = (
        P(SEQ, None),
        P(SEQ, None),
        P(SEQ),
        P(SEQ),
        P(SEQ, None, "head"),
        P(None, "head"),
        P(None, None, "head"),
        P("head", None),
    )
    out_specs = P(SEQ, "head")
    return jax.shard_map(local, mesh=fine, in_specs=in_specs, out_specs=out_specs, check_vma=False)
```

```python
import functools

import jax
import jax.numpy as jnp
from jax import lax
from jax.experimental import pallas as pl
from jax.experimental.pallas import tpu as pltpu
from jax.sharding import Mesh
from jax.sharding import PartitionSpec as P

HD = 64
SPLIT = (("x", 4), ("zh", 4), ("zl", 2), ("yh", 2), ("c", 2))
SEQ = tuple(n for n, _ in SPLIT)
I = ("zl", "yh")
J = ("x", "zh")
NI = 4
NJ = 16
M = 2 * NI
QAT = 4 * M
BIG = 1048576.0
CUT = 65536.0
NEG = -1e30
F32 = jnp.float32
BF16 = jnp.bfloat16


def seq_of(i, j, c):
    size = dict(SPLIT)
    part = {"c": c}
    for names, index in ((I, i), (J, j)):
        for name in reversed(names):
            part[name] = index % size[name]
            index = index // size[name]
    place = 0
    for name, n in SPLIT:
        place = place * n + part[name]
    return place


def iota(shape, dim):
    return lax.broadcasted_iota(jnp.int32, shape, dim)


def onehot(mask):
    return jnp.where(mask, F32(1.0), F32(0.0)).astype(BF16)


def mm(a, b, ca=1, cb=0):
    return lax.dot_general(a, b, (((ca,), (cb,)), ((), ())), preferred_element_type=F32)


def split_kernel(place_ref, own_ref, next_ref, keep_ref, send_ref):
    zl, yh = place_ref[0], place_ref[1]
    row, col = iota((64, 128), 0), iota((64, 128), 1)
    for out_ref, half in ((keep_ref, yh), (send_ref, 1 - yh)):
        b = seq_of(zl * 2 + half, (row // 2) % NJ, row % 2)
        pick = [onehot((col == b) & (row // 32 == r)) for r in range(2)]
        for part in range(2):
            out = mm(pick[0], own_ref[:, part, :]) + mm(pick[1], next_ref[:, part, :])
            out_ref[:, part * 128 : part * 128 + 128] = out.astype(BF16)


def pack_kernel(source_ref, order_ref, avail_ref, queries_ref, wq_ref, out_ref):
    row, col = iota((128, 128), 0), iota((128, 128), 1)
    pick = onehot(jnp.broadcast_to(order_ref[...], (128, 128)) == row)
    relay = onehot(row == seq_of((col // 2) % NI, col // M, col % 2))
    pick = mm(pick, relay).astype(BF16)
    avail = jnp.broadcast_to(avail_ref[...], (128, 128))
    diag = onehot((row == col) & (avail > 0))
    flags = mm(diag, jnp.ones((128, 512), BF16)).astype(BF16)
    live = mm(pick, flags, 0, 0) > 0.5
    rows = jnp.where(live, mm(pick, source_ref[...], 0, 0), F32(BIG)).astype(BF16)
    q = mm(queries_ref[...], wq_ref[...]).astype(BF16)
    q = (q.astype(F32) * (2.0 / HD**0.5)).astype(BF16)
    for j in range(NJ):
        for part in range(4):
            out_ref[j, part * M : part * M + M, :] = rows[
                j * M : j * M + M, part * 128 : part * 128 + 128
            ]
        out_ref[j, QAT : QAT + 128, :] = q


def project_kernel(place_ref, got_ref, pos_ref, wk_ref, wv_ref, out_ref):
    parts = [got_ref[:, part * M : part * M + M, :].reshape(128, 128) for part in range(4)]
    live = parts[0].astype(F32) < CUT
    rows = jnp.concatenate(parts, axis=1)
    zl, yh, c = place_ref[0], place_ref[1], place_ref[2]
    row, col = iota((128, 256), 0), iota((128, 256), 1)
    near = (((row // 2) % 2) ^ yh) * 64 + (((row // 4) % 2) ^ zl) * 32
    relay = onehot(col == (row % 2) * 128 + near + (row // M) * 2 + c)
    pos = mm(relay, pos_ref[...])
    for part, w_ref, mark in ((0, wk_ref, BIG), (1, wv_ref, 0.0)):
        out = mm(rows, w_ref[...]) + pos[:, part * 128 : part * 128 + 128]
        out = jnp.where(live, out, F32(mark)).astype(BF16)
        for i in range(NI):
            out_ref[i, part] = out


def attend_kernel(got_ref, own_ref, other_ref, out_ref, kaug_ref, vaug_ref, *, qb):
    n = NI * 128
    lane = iota((n, 128), 1)
    for side, ref in ((0, own_ref), (1, other_ref)):
        keys = ref[:, 0].reshape(n, 128).astype(F32)
        values = ref[:, 1].reshape(n, 128).astype(F32)
        bad = keys > CUT
        for h in range(2):
            mark = lane == 64 * (1 - h)
            kaug_ref[h, side * n : side * n + n] = jnp.where(
                mark, jnp.where(bad, F32(NEG), F32(0.0)), jnp.where(bad, F32(0.0), keys)
            ).astype(BF16)
            mine = (lane >= 64) if h else (lane < 64)
            vaug_ref[h, side * n : side * n + n] = jnp.where(mine, values, F32(1.0)).astype(BF16)

    lane = iota((qb, 128), 1)
    erow, ecol = iota((16, 128), 0), iota((16, 128), 1)
    pull = onehot((erow < 6) & (ecol == erow % 3 + 64 * (erow // 3)))
    per = qb // 128

    def block(t, carry):
        q = got_ref[pl.ds(t * per, per), QAT : QAT + 128, :].reshape(qb, 128).astype(F32)
        sums, tops = [], []
        for h in range(2):
            mine = (lane >= 64) if h else (lane < 64)
            qh = jnp.where(mine, q, jnp.where(lane == 64 * (1 - h), F32(1.0), F32(0.0)))
            score = mm(qh.astype(BF16), kaug_ref[h], 1, 1)
            top = jnp.max(score, axis=1, keepdims=True)
            weight = jnp.exp(score - top).astype(BF16)
            sums.append(mm(weight, vaug_ref[h]))
            tops.append(top)
        low = lane < 64
        summed = jnp.where(low, sums[0], sums[1])
        total = pltpu.roll(jnp.where(low, sums[1], sums[0]), 64, 1)
        mean = (summed / total).astype(BF16)
        lse = jnp.where(low, tops[0], tops[1]) + jnp.log(total)
        hi = lse.astype(BF16).astype(F32)
        mid = (lse - hi).astype(BF16).astype(F32)
        tail = lse - hi - mid
        which = lane % 64
        piece = jnp.where(which == 0, hi, jnp.where(which == 1, mid, tail)).astype(BF16)
        for u in range(per):
            out_ref[t * per + u, 0:128, :] = mean[u * 128 : u * 128 + 128]
            out_ref[t * per + u, 128:144, :] = mm(pull, piece[u * 128 : u * 128 + 128], 1, 1).astype(BF16)
        return carry

    lax.fori_loop(0, NJ // per, block, 0)


def combine_kernel(got_ref, wo_ref, out_ref):
    row, col = iota((16, 128), 0), iota((16, 128), 1)
    push = onehot(((row < 3) & (col < 64)) | ((row >= 3) & (row < 6) & (col >= 64)))
    lse = [mm(got_ref[j, 128:144, :], push, 0, 0) for j in range(NJ)]
    top = functools.reduce(jnp.maximum, lse)
    total = jnp.zeros((128, 128), F32)
    summed = jnp.zeros((128, 128), F32)
    for j in range(NJ):
        w = jnp.exp(lse[j] - top)
        total = total + w
        summed = summed + w * got_ref[j, 0:128, :].astype(F32)
    attn = (summed / total).astype(BF16)
    terms = mm(attn, wo_ref[...]).astype(BF16)
    for h in range(4):
        out_ref[h] = terms[:, h * 128 : h * 128 + 128]


def vcall(kernel, out, args, scalars=0, scratch=()):
    specs = [pl.BlockSpec(memory_space=pltpu.SMEM)] * scalars
    specs += [pl.BlockSpec(memory_space=pltpu.VMEM)] * (len(args) - scalars)
    outs = jax.tree.map(lambda _: pl.BlockSpec(memory_space=pltpu.VMEM), out)
    return pl.pallas_call(
        kernel,
        out_shape=out,
        in_specs=specs,
        out_specs=outs,
        scratch_shapes=list(scratch),
        compiler_params=pltpu.CompilerParams(vmem_limit_bytes=48 * 1024 * 1024),
    )(*args)


def bf(*shape):
    return jax.ShapeDtypeStruct(shape, BF16)


def swap(x, axes):
    return lax.all_to_all(x, axes, split_axis=0, concat_axis=0, tiled=True)


def local(queries, source, order, avail, pos_table, w_query, w_keyval, w_out):
    place = jnp.stack([lax.axis_index(n).astype(jnp.int32) for n in ("zl", "yh", "c")])
    pair = ((0, 1), (1, 0))
    following = lax.ppermute(pos_table, "zl", pair)
    keep, send = vcall(
        split_kernel, (bf(64, 256), bf(64, 256)), (place, pos_table, following), 1
    )
    pos = jnp.concatenate([keep, lax.ppermute(send, "yh", pair)], axis=0)
    pos = lax.all_gather(pos, "c", axis=0, tiled=True)
    packed = vcall(
        pack_kernel,
        bf(NJ, QAT + 128, 128),
        (source, order.reshape(1, 128), avail.reshape(1, 128), queries, w_query),
    )
    got = swap(packed, J)
    spread = vcall(
        project_kernel,
        bf(NI, 2, 128, 128),
        (place, got, pos, w_keyval[:, 0], w_keyval[:, 1]),
        1,
    )
    own = swap(spread, I)
    other = lax.ppermute(own, "c", pair)
    partial = vcall(
        functools.partial(attend_kernel, qb=256),
        bf(NJ, 144, 128),
        (got, own, other),
        scratch=(pltpu.VMEM((2, 1024, 128), BF16), pltpu.VMEM((2, 1024, 128), BF16)),
    )
    partial = swap(partial, J)
    terms = vcall(combine_kernel, bf(4, 128, 128), (partial, w_out))
    terms = swap(terms, "head")
    own = lax.dynamic_slice_in_dim(queries, lax.axis_index("head") * 128, 128, 1)
    return (own.astype(F32) + terms.astype(F32).sum(axis=0)).astype(BF16)


def solution(mesh):
    fine = Mesh(mesh.devices.reshape(*(n for _, n in SPLIT), 4), (*SEQ, "head"))
    in_specs = (
        P(SEQ, None),
        P(SEQ, None),
        P(SEQ),
        P(SEQ),
        P(SEQ, None, "head"),
        P(None, "head"),
        P(None, None, "head"),
        P("head", None),
    )
    out_specs = P(SEQ, "head")
    return jax.shard_map(local, mesh=fine, in_specs=in_specs, out_specs=out_specs, check_vma=False)
```
